32 devices in a mesh: grp: 4 (over z), ep: 4 (over y, x), tp: 2 (over core).
Axes of the slice: x: 2, y: 2, z: 4, core: 2. Of those that a mesh axis runs over, the one named last changes fastest.
Arguments:
- tokens: bfloat16 [128, 7168], P('ep', 'tp'), may hold values from -6 to 6
- gates: float32 [128, 8], P('ep'), may hold values from 0.05 to 1
- expert_ids: int32 [128, 8], P('ep'), may hold values from 0 to 31, all different within a row; in each aligned block of 16 rows (0 to 15, 16 to 31, ...) at most 8 rows name the same one
- gate_weight: bfloat16 [32, 7168, 2048], P('ep', None, ('grp', 'tp')), may hold values from -0.0625 to 0.0625
- up_weight: bfloat16 [32, 7168, 2048], P('ep', None, ('grp', 'tp')), may hold values from -0.0625 to 0.0625
- down_weight: bfloat16 [32, 2048, 7168], P('ep', ('grp', 'tp')), may hold values from -0.125 to 0.125
Outputs:
- mixed_out: bfloat16 [128, 7168], P('ep', ('grp', 'tp'))
The draws below stay inside these ranges and needn't reach their ends.
Inputs may be any that keep to these rules, and one draw needn't show every extreme that they name: `expert_ids`: within each aligned block of 16 rows, the 8 experts of a row differ, and no expert is named by more than 8 rows; some expert is named by exactly 8 rows in some blocks.
All inputs are finite; a program needn't handle non-finite values.
Results may differ from the reference program's by a relative error of at most 0.013.
Values may be sent and summed in bfloat16 or wider, within the bound.
A program may use at most 192 MiB of HBM per device.

```python
import math
import jax
import jax.numpy as jnp
import numpy as np
from jax import lax

D = 7168
FF = 2048
TOP = 8
EXPERTS = 32
TOK_MB = 16
CAP = 8
TOKENS = 128


def levels(own_key, shape, cuts, smallest, largest):
    gain = 1.0
    for dim, shards_of in cuts:
        steps = jax.random.uniform(jax.random.fold_in(jax.random.fold_in(own_key, 6), dim), (shards_of,), jnp.float32, smallest / len(cuts), largest / len(cuts))
        gain = gain * jnp.repeat(jnp.exp(steps), shape[dim] // shards_of).reshape((-1,) + (1,) * (len(shape) - 1 - dim))
    return gain


def routed_block(stream_key, own, number, rows, number_of, top, most, skew):
    ranking = jax.random.permutation(stream_key, number_of)
    packed, common = shares(number_of, rows * top, most, skew, True), shares(number_of, rows * top, most, skew, False)
    places = jnp.arange(number_of)

    def named(lengths, turn):
        used = int((lengths > 0).sum())
        fixed = max(1, used // 4)
        shifted = fixed + (places - fixed + turn * (used - fixed)) % max(1, number_of - fixed)
        return jnp.zeros((number_of,), jnp.int32).at[ranking[jnp.where(places < fixed, places, shifted)]].set(jnp.asarray(lengths, jnp.int32))

    lengths = jnp.where(number % 4 == 0, named(packed, number // 4), named(common, number - number // 4 - 1))
    mixed = jax.random.permutation(jax.random.fold_in(own, 3), number_of)
    donor, sink = mixed[0:number_of // 2 * 2:2], mixed[1:number_of // 2 * 2:2]
    room = jnp.minimum(lengths[donor] - 1, most - lengths[sink]) // 2
    room = jnp.where((donor == ranking[0]) | (sink == ranking[0]) | (lengths[sink] == 0), 0, jnp.maximum(room, 0))
    shifted = jax.random.randint(jax.random.fold_in(own, 4), (number_of // 2,), 0, 1 << 20) % (room + 1)
    lengths = lengths.at[donor].add(-shifted).at[sink].add(shifted)
    items = jnp.searchsorted(jnp.cumsum(lengths), jnp.arange(rows * top), side="right").astype(jnp.int32)
    grid = items.reshape(top, rows).T
    grid = grid[jax.random.permutation(jax.random.fold_in(own, 1), rows)]
    turn = jax.random.randint(jax.random.fold_in(own, 2), (rows, 1), 0, top)
    return jnp.take_along_axis(grid, (jnp.arange(top)[None, :] + turn) % top, axis=1)


def shares(amount, total, limit, skew, full):
    portions = [(1 << 20) // math.isqrt(grade ** skew) + 1 for grade in range(1, amount + 1)]
    largest = limit if full else min(limit, max(-(-total // amount), total * portions[0] // sum(portions)))
    least = 1 if total - largest >= amount - 1 else 0
    counts, surplus = [largest] + [least] * (amount - 1), total - largest - least * (amount - 1)
    while surplus > 0:
        candidates = [i for i in range(1, amount) if counts[i] < largest] or [i for i in range(1, amount) if counts[i] < limit]
        mass, remaining = sum([portions[i] for i in candidates]), surplus
        for i in candidates:
            extra = min(limit - counts[i], max(1, remaining * portions[i] // mass), surplus)
            counts[i] = counts[i] + extra
            surplus = surplus - extra
    return np.array(counts)


def scatter_about(rng, shape, deviation, most, pieces=(), kind=jnp.bfloat16):
    entries = deviation * jax.random.normal(rng, shape, jnp.float32)
    if pieces:
        entries = entries * levels(rng, shape, pieces, -0.22, 0.18)
    return jnp.clip(entries, -most, most).astype(kind)


def setup_inputs(seed: int = 0) -> dict:
    key_of = jax.random.split(jax.random.key(seed), 7)
    tokens = scatter_about(key_of[0], (TOKENS, D), 1.0, 6.0, ((0, 4), (1, 2)))
    gates = jnp.clip(jnp.exp(math.log(1.0) - 2.9957323 * jax.random.uniform(key_of[1], (TOKENS, TOP), jnp.float32) ** levels(key_of[1], (TOKENS, TOP), ((0, 4),), -0.2, 0.2)), 0.05, 1.0)
    expert_ids_keys = jax.random.split(jax.random.fold_in(key_of[2], 1), TOKENS // TOK_MB)
    expert_ids_turns = jax.random.permutation(jax.random.fold_in(key_of[2], 3), TOKENS // TOK_MB)
    expert_ids = jax.vmap(lambda own, number: routed_block(jax.random.fold_in(key_of[2], 2), own, number, TOK_MB, EXPERTS, TOP, CAP, 2))(expert_ids_keys, expert_ids_turns).reshape((TOKENS, TOP))
    gate_weight = scatter_about(key_of[3], (EXPERTS, D, FF), D ** -0.5, 0.0625, ((0, 4), (2, 8)))
    up_weight = scatter_about(key_of[4], (EXPERTS, D, FF), D ** -0.5, 0.0625, ((0, 4), (2, 8)))
    down_weight = scatter_about(key_of[5], (EXPERTS, FF, D), FF ** -0.5, 0.125, ((0, 4), (1, 8)))
    return dict(tokens=tokens, gates=gates, expert_ids=expert_ids, gate_weight=gate_weight, up_weight=up_weight, down_weight=down_weight)


def reference(tokens, gates, expert_ids, gate_weight, up_weight, down_weight):
    blocks = TOKENS // TOK_MB
    assigned = expert_ids.reshape(blocks, TOK_MB * TOP).astype(jnp.int32)
    labels = jnp.arange(EXPERTS, dtype=jnp.int32)
    onehot = (assigned[:, :, None] == labels[None, None, :]).astype(jnp.int32)
    before = jnp.cumsum(onehot, axis=1) - onehot
    slot = jnp.sum(before * onehot, axis=2).astype(jnp.int32)
    position = jnp.arange(TOK_MB * TOP, dtype=jnp.int32)
    block_rows = jnp.arange(blocks, dtype=jnp.int32)
    owner_row = (block_rows[:, None] * TOK_MB + position[None, :] // TOP).astype(jnp.int32)
    block_index = jnp.broadcast_to(block_rows[:, None], assigned.shape)
    table = jnp.full((blocks, EXPERTS, CAP), TOKENS, jnp.int32).at[block_index, assigned, slot].set(owner_row)
    weight_table = jnp.zeros((blocks, EXPERTS, CAP), jnp.float32).at[block_index, assigned, slot].set(
        gates.reshape(blocks, TOK_MB * TOP).astype(jnp.float32))
    padded = jnp.concatenate([tokens, jnp.zeros((1, D), tokens.dtype)], axis=0)

    def apply(total, expert):
        picked = table[:, expert].reshape(-1)
        scale = weight_table[:, expert].reshape(-1)
        rows = padded[picked].astype(jnp.float32)
        gate = jnp.dot(rows, gate_weight[expert].astype(jnp.float32), preferred_element_type=jnp.float32)
        upper = jnp.dot(rows, up_weight[expert].astype(jnp.float32), preferred_element_type=jnp.float32)
        hidden = lax.optimization_barrier((jax.nn.silu(gate) * upper).astype(jnp.bfloat16)).astype(jnp.float32)
        result = jnp.dot(hidden, down_weight[expert].astype(jnp.float32), preferred_element_type=jnp.float32)
        result = lax.optimization_barrier(result.astype(jnp.bfloat16)).astype(jnp.float32)
        return total.at[picked].add(scale[:, None] * result), None

    start = jnp.zeros((TOKENS + 1, D), jnp.float32)
    total, unused = lax.scan(apply, start, jnp.arange(EXPERTS, dtype=jnp.int32))
    return total[:TOKENS].astype(jnp.bfloat16)
```

```python
import functools

import jax
import jax.numpy as jnp
from jax import lax
from jax.experimental import pallas as pl
from jax.experimental.pallas import tpu as pltpu
from jax.sharding import PartitionSpec as P

MESH = pl.DeviceIdType.MESH
EXPERT_SLOTS = 5
DOWN_SLOTS = 4
ROW_BLOCK = 256


def kernel(
    ep, grp, tp,
    tok, gates, ids, wg, wu, wd, out,
    x, gall, iall, wgb, wub, wdb, hid, own, tsend, trecv, psend, xyrecv, zsend, zrecv,
    w_sem, d_sem, loc_sem, ag_s, ag_r, gt_s, gt_r, id_s, id_r, f_s, f_r,
    t_s, t_r, xy_s, xy_r, z_s, z_r,
):
    me_ep, me_grp, me_tp = lax.axis_index("ep"), lax.axis_index("grp"), lax.axis_index("tp")
    mate = 1 - me_tp
    experts, width, units = wg.shape
    rows, half = tok.shape
    share = out.shape[1]
    total = rows * ep
    slots = wgb.shape[0]
    down_slots = wdb.shape[0]
    chunks = grp * tp

    def at_rows(index):
        return pl.ds(pl.multiple_of(index * rows, rows), rows)

    def expert_copies(e):
        s = lax.rem(e, slots)
        return (
            pltpu.make_async_copy(wg.at[e], wgb.at[s], w_sem.at[s, 0]),
            pltpu.make_async_copy(wu.at[e], wub.at[s], w_sem.at[s, 1]),
        )

    def group_of(i):
        return lax.rem(me_grp + 1 + i, grp)

    def down_copy(c):
        s = lax.rem(c, down_slots)
        i, second = c // 2, lax.rem(c, 2)
        column = group_of(i) * 2 + lax.rem(mate + second, 2)
        return pltpu.make_async_copy(
            wd.at[:, pl.ds(pl.multiple_of(column * share, 128), share)], wdb.at[s], d_sem.at[s]
        )

    def start_expert(e):
        for copy in expert_copies(e):
            copy.start()

    for e in range(slots):
        start_expert(jnp.int32(e))
    own_rows = pltpu.make_async_copy(tok, x.at[me_tp, at_rows(me_ep)], loc_sem.at[0])
    own_rows.start()

    barrier = pltpu.get_barrier_semaphore()

    @pl.loop(1, ep)
    def _(d):
        pl.semaphore_signal(
            barrier, inc=1, device_id={"ep": lax.rem(me_ep + d, ep)}, device_id_type=MESH
        )

    @pl.loop(1, grp)
    def _(d):
        pl.semaphore_signal(
            barrier, inc=1, device_id={"grp": lax.rem(me_grp + d, grp)}, device_id_type=MESH
        )

    pl.semaphore_signal(barrier, inc=1, device_id={"tp": mate}, device_id_type=MESH)
    pl.semaphore_wait(barrier, ep + grp - 1)

    def gather_copies(d):
        to = {"ep": lax.rem(me_ep + d, ep)}
        mine = at_rows(me_ep)
        return (
            pltpu.make_async_remote_copy(
                tok, x.at[me_tp, mine], ag_s.at[d], ag_r.at[d], to, MESH
            ),
            pltpu.make_async_remote_copy(
                gates, gall.at[me_ep], gt_s.at[d], gt_r.at[d], to, MESH
            ),
            pltpu.make_async_remote_copy(
                ids, iall.at[me_ep], id_s.at[d], id_r.at[d], to, MESH
            ),
        )

    def pass_on(d):
        where = x.at[me_tp, at_rows(lax.rem(me_ep - d + ep, ep))]
        return pltpu.make_async_remote_copy(
            where, where, f_s.at[d], f_r.at[d], {"tp": mate}, MESH
        )

    def pass_own():
        return pltpu.make_async_remote_copy(
            tok, x.at[me_tp, at_rows(me_ep)], f_s.at[0], f_r.at[0], {"tp": mate}, MESH
        )

    @pl.loop(1, ep)
    def _(d):
        for copy in gather_copies(d):
            copy.start()

    pass_own().start()
    for c in range(down_slots):
        down_copy(jnp.int32(c)).start()
    gall[me_ep] = gates[...]
    iall[me_ep] = ids[...]

    @pl.loop(1, ep)
    def _(d):
        gather_copies(d)[0].wait_recv()
        pass_on(d).start()

    own_rows.wait()
    pass_own().wait_recv()

    @pl.loop(1, ep)
    def _(d):
        pass_on(d).wait_recv()
        for copy in gather_copies(d)[1:]:
            copy.wait_recv()

    block = min(total, ROW_BLOCK)

    def by_rows(body):
        if block == total:
            body(0)
        else:
            pl.loop(0, total // block)(lambda b: body(pl.multiple_of(b * block, block)))

    per_block = block // rows

    @pl.loop(0, experts)
    def _(e):
        s = lax.rem(e, slots)
        for copy in expert_copies(e):
            copy.wait()
        number = me_ep * experts + e

        def body(start):
            def project(w):
                parts = [
                    jnp.dot(
                        x[t, pl.ds(start, block), :],
                        w[s, t * half : (t + 1) * half, :],
                        preferred_element_type=jnp.float32,
                    )
                    for t in range(tp)
                ]
                return functools.reduce(jnp.add, parts)

            gate, up = project(wgb), project(wub)
            first = start // rows
            chosen = iall[pl.ds(first, per_block)].reshape(block, ids.shape[1])
            weights = gall[pl.ds(first, per_block)].reshape(block, ids.shape[1])
            scale = jnp.sum(
                jnp.where(chosen == number, weights, 0.0), axis=1, keepdims=True
            )
            value = gate / (1.0 + jnp.exp(-gate)) * up * scale
            hid[pl.ds(start, block), pl.ds(pl.multiple_of(e * units, units), units)] = (
                value.astype(hid.dtype)
            )

        by_rows(body)

        @pl.when(e + slots < experts)
        def _():
            start_expert(e + slots)

    def project_down(c, target):
        s = lax.rem(c, down_slots)
        down_copy(c).wait()

        def body(start):
            where = pl.ds(start, block)
            target[where, :] = jnp.dot(
                hid[where, :], wdb[s], preferred_element_type=jnp.float32
            ).astype(target.dtype)

        by_rows(body)

        @pl.when(c + down_slots < chunks)
        def _():
            down_copy(c + down_slots).start()

    def to_mate(i):
        return pltpu.make_async_remote_copy(
            tsend.at[i], trecv.at[i], t_s.at[i], t_r.at[i], {"tp": mate}, MESH
        )

    def to_source(i, d):
        peer = lax.rem(me_ep + d, ep)
        return pltpu.make_async_remote_copy(
            psend.at[i, at_rows(peer)], xyrecv.at[i, d], xy_s.at[i, d], xy_r.at[i, d],
            {"ep": peer}, MESH,
        )

    def to_group(i):
        return pltpu.make_async_remote_copy(
            zsend.at[i], zrecv.at[i], z_s.at[i], z_r.at[i], {"grp": group_of(i)}, MESH
        )

    def add_mate(i):
        to_mate(i).wait_recv()

        def body(start):
            where = pl.ds(start, block)
            psend[i, where, :] = (own[where, :] + trecv[i, where, :].astype(jnp.float32)).astype(
                psend.dtype
            )

        by_rows(body)
        pl.loop(1, ep)(lambda d: to_source(i, d).start())

    def add_sources(i):
        pl.loop(1, ep)(lambda d: to_source(i, d).wait_recv())
        mine = psend[i, at_rows(me_ep), :].astype(jnp.float32)
        return lax.fori_loop(
            1, ep, lambda d, acc: acc + xyrecv[i, d].astype(jnp.float32), mine
        )

    def add_and_send(i):
        zsend[i] = add_sources(i).astype(zsend.dtype)
        to_group(i).start()

    @pl.loop(0, grp)
    def _(i):
        project_down(2 * i, tsend.at[i])
        to_mate(i).start()

        @pl.when(i > 0)
        def _():
            add_mate(i - 1)

        project_down(2 * i + 1, own)

        @pl.when(i > 0)
        def _():
            add_and_send(i - 1)

    add_mate(grp - 1)
    result = add_sources(grp - 1)
    for i in range(grp - 1):
        to_group(i).wait_recv()
        result = result + zrecv[i].astype(jnp.float32)
    out[...] = result.astype(out.dtype)

    pass_own().wait_send()

    @pl.loop(1, ep)
    def _(d):
        for copy in gather_copies(d):
            copy.wait_send()
        pass_on(d).wait_send()

    @pl.loop(0, grp)
    def _(i):
        to_mate(i).wait_send()
        pl.loop(1, ep)(lambda d: to_source(i, d).wait_send())

    pl.loop(0, grp - 1)(lambda i: to_group(i).wait_send())


def local(tokens, gates, expert_ids, gate_weight, up_weight, down_weight):
    ep, grp, tp = lax.axis_size("ep"), lax.axis_size("grp"), lax.axis_size("tp")
    rows, half = tokens.shape
    experts, width, units = gate_weight.shape
    share = width // (grp * tp)
    total = rows * ep
    top = gates.shape[1]
    slots = min(EXPERT_SLOTS, experts)
    bf16, f32 = jnp.bfloat16, jnp.float32
    down = down_weight.reshape(experts * units, width)
    down_slots = min(DOWN_SLOTS, grp * tp)
    dma = pltpu.SemaphoreType.DMA
    vmem = pl.BlockSpec(memory_space=pltpu.VMEM)
    hbm = pl.BlockSpec(memory_space=pl.ANY)
    return pl.pallas_call(
        functools.partial(kernel, ep, grp, tp),
        out_shape=jax.ShapeDtypeStruct((rows, share), bf16),
        in_specs=[hbm, vmem, vmem, hbm, hbm, hbm],
        out_specs=vmem,
        scratch_shapes=[
            pltpu.VMEM((tp, total, half), bf16),
            pltpu.VMEM((ep, rows, top), f32),
            pltpu.VMEM((ep, rows, top), jnp.int32),
            pltpu.VMEM((slots, width, units), bf16),
            pltpu.VMEM((slots, width, units), bf16),
            pltpu.VMEM((down_slots, experts * units, share), bf16),
            pltpu.VMEM((total, experts * units), bf16),
            pltpu.VMEM((total, share), f32),
            pltpu.VMEM((grp, total, share), bf16),
            pltpu.VMEM((grp, total, share), bf16),
            pltpu.VMEM((grp, total, share), bf16),
            pltpu.VMEM((grp, ep, rows, share), bf16),
            pltpu.VMEM((grp, rows, share), bf16),
            pltpu.VMEM((grp, rows, share), bf16),
            dma((slots, 2)), dma((down_slots,)), dma((1,)),
            dma((ep,)), dma((ep,)), dma((ep,)), dma((ep,)), dma((ep,)), dma((ep,)),
            dma((ep,)), dma((ep,)),
            dma((grp,)), dma((grp,)), dma((grp, ep)), dma((grp, ep)), dma((grp,)), dma((grp,)),
        ],
        compiler_params=pltpu.CompilerParams(
            collective_id=0, has_side_effects=True, vmem_limit_bytes=66_000_000
        ),
    )(tokens, gates, expert_ids, gate_weight, up_weight, down)


def solution(mesh):
    placed = (
        P("ep", "tp"),
        P("ep", None),
        P("ep", None),
        P("ep", None, ("grp", "tp")),
        P("ep", None, ("grp", "tp")),
        P("ep", ("grp", "tp"), None),
    )
    return jax.shard_map(
        local, mesh=mesh, in_specs=placed, out_specs=P("ep", ("grp", "tp")), check_vma=False
    )
```

```python
import functools

import jax
import jax.numpy as jnp
from jax import lax
from jax.experimental import pallas as pl
from jax.experimental.pallas import tpu as pltpu
from jax.sharding import PartitionSpec as P

MESH = pl.DeviceIdType.MESH
EXPERT_SLOTS = 5
DOWN_SLOTS = 4
ROW_BLOCK = 256
PIECES = 2


def kernel(
    ep, grp, tp,
    tok, gates, ids, wg, wu, wd, out,
    x, gall, iall, wgb, wub, wdb, hid, own, tsend, trecv, psend, xyrecv, zsend, zrecv,
    w_sem, d_sem, loc_sem, ag_s, ag_r, gt_s, gt_r, id_s, id_r, f_s, f_r,
    t_s, t_r, xy_s, xy_r, z_s, z_r,
):
    me_ep, me_grp, me_tp = lax.axis_index("ep"), lax.axis_index("grp"), lax.axis_index("tp")
    mate = 1 - me_tp
    experts, width, units = wg.shape
    rows, half = tok.shape
    share = out.shape[1]
    total = rows * ep
    slots = wgb.shape[0]
    down_slots = wdb.shape[0]
    chunks = grp * tp

    def at_rows(index):
        return pl.ds(pl.multiple_of(index * rows, rows), rows)

    def expert_copies(e):
        s = lax.rem(e, slots)
        return (
            pltpu.make_async_copy(wg.at[e], wgb.at[s], w_sem.at[s, 0]),
            pltpu.make_async_copy(wu.at[e], wub.at[s], w_sem.at[s, 1]),
        )

    def group_of(i):
        return lax.rem(me_grp + 1 + i, grp)

    def down_copy(c):
        s = lax.rem(c, down_slots)
        i, second = c // 2, lax.rem(c, 2)
        column = group_of(i) * 2 + lax.rem(mate + second, 2)
        return pltpu.make_async_copy(
            wd.at[:, pl.ds(pl.multiple_of(column * share, 128), share)], wdb.at[s], d_sem.at[s]
        )

    def start_expert(e):
        for copy in expert_copies(e):
            copy.start()

    for e in range(slots):
        start_expert(jnp.int32(e))
    own_rows = pltpu.make_async_copy(tok, x.at[me_tp, at_rows(me_ep)], loc_sem.at[0])
    own_rows.start()

    barrier = pltpu.get_barrier_semaphore()

    @pl.loop(1, ep)
    def _(d):
        pl.semaphore_signal(
            barrier, inc=1, device_id={"ep": lax.rem(me_ep + d, ep)}, device_id_type=MESH
        )

    @pl.loop(1, grp)
    def _(d):
        pl.semaphore_signal(
            barrier, inc=1, device_id={"grp": lax.rem(me_grp + d, grp)}, device_id_type=MESH
        )

    pl.semaphore_signal(barrier, inc=1, device_id={"tp": mate}, device_id_type=MESH)
    pl.semaphore_wait(barrier, ep + grp - 1)

    piece = half // PIECES

    def gather_piece(d, p):
        cols = pl.ds(p * piece, piece)
        return pltpu.make_async_remote_copy(
            tok.at[:, cols], x.at[me_tp, at_rows(me_ep), cols], ag_s.at[d, p], ag_r.at[d, p],
            {"ep": lax.rem(me_ep + d, ep)}, MESH,
        )

    def gather_routes(d):
        to = {"ep": lax.rem(me_ep + d, ep)}
        return (
            pltpu.make_async_remote_copy(
                gates, gall.at[me_ep], gt_s.at[d], gt_r.at[d], to, MESH
            ),
            pltpu.make_async_remote_copy(
                ids, iall.at[me_ep], id_s.at[d], id_r.at[d], to, MESH
            ),
        )

    def pass_on(d, p):
        where = x.at[me_tp, at_rows(lax.rem(me_ep - d + ep, ep)), pl.ds(p * piece, piece)]
        return pltpu.make_async_remote_copy(
            where, where, f_s.at[d, p], f_r.at[d, p], {"tp": mate}, MESH
        )

    def pass_own():
        return pltpu.make_async_remote_copy(
            tok, x.at[me_tp, at_rows(me_ep)], f_s.at[0, 0], f_r.at[0, 0], {"tp": mate}, MESH
        )

    for p in range(PIECES):
        pl.loop(1, ep)(lambda d: gather_piece(d, p).start())

    @pl.loop(1, ep)
    def _(d):
        for copy in gather_routes(d):
            copy.start()

    pass_own().start()
    for c in range(down_slots):
        down_copy(jnp.int32(c)).start()
    gall[me_ep] = gates[...]
    iall[me_ep] = ids[...]

    for p in range(PIECES):

        @pl.loop(1, ep)
        def _(d):
            gather_piece(d, p).wait_recv()
            pass_on(d, p).start()

    own_rows.wait()
    pass_own().wait_recv()

    @pl.loop(1, ep)
    def _(d):
        for p in range(PIECES):
            pass_on(d, p).wait_recv()
        for copy in gather_routes(d):
            copy.wait_recv()

    block = min(total, ROW_BLOCK)

    def by_rows(body):
        if block == total:
            body(0)
        else:
            pl.loop(0, total // block)(lambda b: body(pl.multiple_of(b * block, block)))

    per_block = block // rows

    @pl.loop(0, experts)
    def _(e):
        s = lax.rem(e, slots)
        for copy in expert_copies(e):
            copy.wait()
        number = me_ep * experts + e

        def body(start):
            def project(w):
                parts = [
                    jnp.dot(
                        x[t, pl.ds(start, block), :],
                        w[s, t * half : (t + 1) * half, :],
                        preferred_element_type=jnp.float32,
                    )
                    for t in range(tp)
                ]
                return functools.reduce(jnp.add, parts)

            gate, up = project(wgb), project(wub)
            first = start // rows
            chosen = iall[pl.ds(first, per_block)].reshape(block, ids.shape[1])
            weights = gall[pl.ds(first, per_block)].reshape(block, ids.shape[1])
            scale = jnp.sum(
                jnp.where(chosen == number, weights, 0.0), axis=1, keepdims=True
            )
            value = gate / (1.0 + jnp.exp(-gate)) * up * scale
            hid[pl.ds(start, block), pl.ds(pl.multiple_of(e * units, units), units)] = (
                value.astype(hid.dtype)
            )

        by_rows(body)

        @pl.when(e + slots < experts)
        def _():
            start_expert(e + slots)

    def project_down(c, target):
        s = lax.rem(c, down_slots)
        down_copy(c).wait()

        def body(start):
            where = pl.ds(start, block)
            target[where, :] = jnp.dot(
                hid[where, :], wdb[s], preferred_element_type=jnp.float32
            ).astype(target.dtype)

        by_rows(body)

        @pl.when(c + down_slots < chunks)
        def _():
            down_copy(c + down_slots).start()

    def to_mate(i):
        return pltpu.make_async_remote_copy(
            tsend.at[i], trecv.at[i], t_s.at[i], t_r.at[i], {"tp": mate}, MESH
        )

    def to_source(i, d):
        peer = lax.rem(me_ep + d, ep)
        return pltpu.make_async_remote_copy(
            psend.at[i, at_rows(peer)], xyrecv.at[i, d], xy_s.at[i, d], xy_r.at[i, d],
            {"ep": peer}, MESH,
        )

    def to_group(i):
        return pltpu.make_async_remote_copy(
            zsend.at[i], zrecv.at[i], z_s.at[i], z_r.at[i], {"grp": group_of(i)}, MESH
        )

    def add_mate(i):
        to_mate(i).wait_recv()

        def body(start):
            where = pl.ds(start, block)
            psend[i, where, :] = (own[where, :] + trecv[i, where, :].astype(jnp.float32)).astype(
                psend.dtype
            )

        by_rows(body)
        pl.loop(1, ep)(lambda d: to_source(i, d).start())

    def add_sources(i):
        pl.loop(1, ep)(lambda d: to_source(i, d).wait_recv())
        mine = psend[i, at_rows(me_ep), :].astype(jnp.float32)
        return lax.fori_loop(
            1, ep, lambda d, acc: acc + xyrecv[i, d].astype(jnp.float32), mine
        )

    def add_and_send(i):
        zsend[i] = add_sources(i).astype(zsend.dtype)
        to_group(i).start()

    @pl.loop(0, grp)
    def _(i):
        project_down(2 * i, tsend.at[i])
        to_mate(i).start()

        @pl.when(i > 0)
        def _():
            add_mate(i - 1)

        project_down(2 * i + 1, own)

        @pl.when(i > 1)
        def _():
            add_and_send(i - 2)

    add_mate(grp - 1)
    if grp > 1:
        add_and_send(grp - 2)
    result = add_sources(grp - 1)
    for i in range(grp - 1):
        to_group(i).wait_recv()
        result = result + zrecv[i].astype(jnp.float32)
    out[...] = result.astype(out.dtype)

    pass_own().wait_send()

    @pl.loop(1, ep)
    def _(d):
        for copy in gather_routes(d):
            copy.wait_send()
        for p in range(PIECES):
            gather_piece(d, p).wait_send()
            pass_on(d, p).wait_send()

    @pl.loop(0, grp)
    def _(i):
        to_mate(i).wait_send()
        pl.loop(1, ep)(lambda d: to_source(i, d).wait_send())

    pl.loop(0, grp - 1)(lambda i: to_group(i).wait_send())


def local(tokens, gates, expert_ids, gate_weight, up_weight, down_weight):
    ep, grp, tp = lax.axis_size("ep"), lax.axis_size("grp"), lax.axis_size("tp")
    rows, half = tokens.shape
    experts, width, units = gate_weight.shape
    share = width // (grp * tp)
    total = rows * ep
    top = gates.shape[1]
    slots = min(EXPERT_SLOTS, experts)
    bf16, f32 = jnp.bfloat16, jnp.float32
    down = down_weight.reshape(experts * units, width)
    down_slots = min(DOWN_SLOTS, grp * tp)
    dma = pltpu.SemaphoreType.DMA
    vmem = pl.BlockSpec(memory_space=pltpu.VMEM)
    hbm = pl.BlockSpec(memory_space=pl.ANY)
    return pl.pallas_call(
        functools.partial(kernel, ep, grp, tp),
        out_shape=jax.ShapeDtypeStruct((rows, share), bf16),
        in_specs=[hbm, vmem, vmem, hbm, hbm, hbm],
        out_specs=vmem,
        scratch_shapes=[
            pltpu.VMEM((tp, total, half), bf16),
            pltpu.VMEM((ep, rows, top), f32),
            pltpu.VMEM((ep, rows, top), jnp.int32),
            pltpu.VMEM((slots, width, units), bf16),
            pltpu.VMEM((slots, width, units), bf16),
            pltpu.VMEM((down_slots, experts * units, share), bf16),
            pltpu.VMEM((total, experts * units), bf16),
            pltpu.VMEM((total, share), f32),
            pltpu.VMEM((grp, total, share), bf16),
            pltpu.VMEM((grp, total, share), bf16),
            pltpu.VMEM((grp, total, share), bf16),
            pltpu.VMEM((grp, ep, rows, share), bf16),
            pltpu.VMEM((grp, rows, share), bf16),
            pltpu.VMEM((grp, rows, share), bf16),
            dma((slots, 2)), dma((down_slots,)), dma((1,)),
            dma((ep, PIECES)), dma((ep, PIECES)), dma((ep,)), dma((ep,)), dma((ep,)), dma((ep,)),
            dma((ep, PIECES)), dma((ep, PIECES)),
            dma((grp,)), dma((grp,)), dma((grp, ep)), dma((grp, ep)), dma((grp,)), dma((grp,)),
        ],
        compiler_params=pltpu.CompilerParams(
            collective_id=0, has_side_effects=True, vmem_limit_bytes=66_000_000
        ),
    )(tokens, gates, expert_ids, gate_weight, up_weight, down)


def solution(mesh):
    placed = (
        P("ep", "tp"),
        P("ep", None),
        P("ep", None),
        P("ep", None, ("grp", "tp")),
        P("ep", None, ("grp", "tp")),
        P("ep", ("grp", "tp"), None),
    )
    return jax.shard_map(
        local, mesh=mesh, in_specs=placed, out_specs=P("ep", ("grp", "tp")), check_vma=False
    )
```
